32 devices in a mesh: depth: 8 (over z, x), imgy: 2 (over y), imgx: 2 (over core).
Axes of the slice: x: 2, y: 2, z: 4, core: 2. Of those that a mesh axis runs over, the one named last changes fastest.
Arguments:
- volume: bfloat16 [128, 512, 1024], P('depth', 'imgy', 'imgx'), may hold values from -6 to 6
- tf_centers: float32 [4], replicated, may hold values from -2 to 2
- tf_widths: float32 [4], replicated, may hold values from 0.4 to 1.5
- tf_colors: float32 [3, 4], replicated, may hold values from 0.2 to 3
- tf_opacity: float32 [4], replicated, may hold values from 0.3 to 3
Outputs:
- frame: float32 [4, 2, 256, 1024], P(None, 'imgy', 'depth', 'imgx')
The draws below stay inside these ranges and needn't reach their ends.
All inputs are finite; a program needn't handle non-finite values.
Results may differ from the reference program's by a relative error of at most 0.0003.
Values may be sent and summed in bfloat16 or wider, within the bound.
A program may use at most 64 MiB of HBM per device.

```python
import math
import jax
import jax.numpy as jnp
from jax import lax

BY = 256
BUMPS = 4
Z = 128
Y = 512
X = 1024
TILES_Y = 2


def shard_levels(rng, dims, pieces, least, high):
    gain, own = 1.0, jax.random.fold_in(rng, 6)
    for position, parts in pieces:
        steps = jnp.exp(jax.random.uniform(jax.random.fold_in(own, position), (parts,), jnp.float32, least / len(pieces), high / len(pieces)))
        gain = gain * jnp.repeat(steps, dims[position] // parts).reshape([-1 if axis == position else 1 for axis in range(len(dims))])
    return gain


def gaussian(rng, extent, deviation, limit, shards=(), kind=jnp.bfloat16):
    result = jax.random.normal(rng, extent, jnp.float32) * deviation
    if len(shards) > 0:
        result = shard_levels(rng, extent, shards, -0.22, 0.18) * result
    return jnp.clip(result, min=-limit, max=limit).astype(kind)


def setup_inputs(seed: int = 0) -> dict:
    key_list = jax.random.split(jax.random.key(seed), 6)
    volume = gaussian(key_list[0], (Z, Y, X), 1.0, 6.0, ((0, 8), (1, 2), (2, 2)))
    tf_centers = jnp.clip(jax.random.uniform(key_list[1], (BUMPS,), jnp.float32, -2.0, 2.0), -2.0, 2.0)
    tf_widths = jnp.clip(jnp.exp(jax.random.uniform(key_list[2], (BUMPS,), jnp.float32, math.log(0.4), math.log(1.5))), 0.4, 1.5)
    tf_colors = jnp.clip(jax.random.uniform(key_list[3], (3, BUMPS), jnp.float32, 0.2, 3.0), 0.2, 3.0)
    tf_opacity = jnp.clip(jnp.exp(jax.random.uniform(key_list[4], (BUMPS,), jnp.float32, math.log(0.3), math.log(3.0))), 0.3, 3.0)
    return {"volume": volume, "tf_centers": tf_centers, "tf_widths": tf_widths, "tf_colors": tf_colors, "tf_opacity": tf_opacity}


def shading(middle, grad_depth, grad_rows, grad_cols, tf_centers, tf_widths, tf_colors, tf_opacity, ray_step):
    extinction = jnp.zeros_like(middle)
    emission = [jnp.zeros_like(middle), jnp.zeros_like(middle), jnp.zeros_like(middle)]
    for bump_index in range(tf_centers.shape[0]):
        offset = (middle - tf_centers[bump_index]) / tf_widths[bump_index]
        profile = jnp.exp(-offset * offset)
        extinction = extinction + tf_opacity[bump_index] * profile
        for channel in range(3):
            emission[channel] = emission[channel] + tf_colors[channel, bump_index] * profile
    gradient_norm = jnp.sqrt(grad_depth * grad_depth + grad_rows * grad_rows + grad_cols * grad_cols + 0.25)
    lighting = 0.3 + 0.7 * jnp.abs(grad_depth) / gradient_norm
    passing = jnp.exp(-ray_step * extinction)
    weight = (1.0 - passing) * lighting
    glowing = jnp.stack([emitted * weight for emitted in emission])
    return (glowing, passing)

def reference(volume, tf_centers, tf_widths, tf_colors, tf_opacity):
    depth_count = volume.shape[0]
    ray_step = 1.5 / depth_count
    rows_all = volume.shape[1]
    cols_all = volume.shape[2]

    def march_layer(carried, layer_index):
        color_sum, passed = carried
        middle = lax.dynamic_index_in_dim(volume, layer_index, 0, keepdims=False).astype(jnp.float32)
        before_index = jnp.maximum(layer_index - 1, 0).astype(jnp.int32)
        after_index = jnp.minimum(layer_index + 1, depth_count - 1).astype(jnp.int32)
        before = lax.dynamic_index_in_dim(volume, before_index, 0, keepdims=False).astype(jnp.float32)
        after = lax.dynamic_index_in_dim(volume, after_index, 0, keepdims=False).astype(jnp.float32)
        before = jnp.where(layer_index > 0, before, jnp.float32(0.0))
        after = jnp.where(layer_index < depth_count - 1, after, jnp.float32(0.0))
        grad_depth = 0.5 * (after - before)
        side = jnp.pad(middle, 1)
        grad_rows = 0.5 * (side[2:, 1:-1] - side[:-2, 1:-1])
        grad_cols = 0.5 * (side[1:-1, 2:] - side[1:-1, :-2])
        glowing, passing = shading(middle, grad_depth, grad_rows, grad_cols, tf_centers, tf_widths, tf_colors, tf_opacity, ray_step)
        return ((color_sum + passed[None] * glowing, passed * passing), None)
    start = (jnp.zeros((3, rows_all, cols_all), jnp.float32), jnp.ones((rows_all, cols_all), jnp.float32))
    final, unused = lax.scan(march_layer, start, jnp.arange(depth_count, dtype=jnp.int32))
    color_sum, passed = final
    frame = jnp.concatenate([color_sum, (1.0 - passed)[None]], axis=0)
    return frame.reshape(4, TILES_Y, BY, cols_all)
```

```python
import functools
import math

import jax
import jax.numpy as jnp
from jax import lax
from jax.experimental import pallas as pl
from jax.experimental.pallas import tpu as pltpu
from jax.sharding import PartitionSpec as P

LOG2E = math.log2(math.e)
RS = 16
CS = 128
CH = 32


def fill_bands(dcol, drow):
    k = lax.broadcasted_iota(jnp.int32, dcol.shape, 0)
    j = lax.broadcasted_iota(jnp.int32, dcol.shape, 1)
    dcol[...] = jnp.where(k == j + CS + 1, 1.0, jnp.where(k == j + CS - 1, -1.0, 0.0)).astype(dcol.dtype)
    i = lax.broadcasted_iota(jnp.int32, drow.shape, 0)
    k = lax.broadcasted_iota(jnp.int32, drow.shape, 1)
    drow[...] = jnp.where(k == i + RS + 1, 1.0, jnp.where(k == i + RS - 1, -1.0, 0.0)).astype(drow.dtype)


def tables(layers_all, centers, widths, colors, opacity):
    scale = 1.5 / layers_all * LOG2E
    cen, quad, off = [], [], []
    mat = [[], [], []]
    for k in range(4):
        w = jnp.full((8, 128), widths[k], jnp.float32)
        o = jnp.full((8, 128), opacity[k], jnp.float32) * scale
        cen.append(jnp.full((8, 128), centers[k], jnp.float32))
        quad.append(-LOG2E / (w * w))
        off.append(jnp.log2(o))
        for c in range(3):
            mat[c].append(0.7 * colors[c, k] / o)
    return cen, quad, off, mat


def march_chunk(r0, ext, cscr, rscr, dcol, drow, tab, store):
    layers = ext.shape[0] - 2
    cols = ext.shape[2] - 2 * CS
    for h in range(cols // 256):
        left = ext[1 : layers + 1, pl.ds(r0 + RS, CH), h * 256 : h * 256 + 512].reshape(layers * CH, 512)
        cscr[:, :, h * 256 : h * 256 + 256] = jnp.dot(
            left, dcol[...], preferred_element_type=jnp.float32
        ).reshape(layers, CH, 256)
    for z in range(layers):
        rscr[z] = jnp.dot(
            drow[...], ext[1 + z, pl.ds(r0, CH + 2 * RS), CS : CS + cols], preferred_element_type=jnp.float32
        )
    cen8, quad8, off8, mat8 = tab
    two = lambda v: jnp.concatenate([v, v], axis=0)
    tiles = cols // 128

    def tile(t, _):
        q0 = pl.multiple_of(t // tiles * 16, 16)
        l0 = pl.multiple_of(t % tiles * 128, 128)
        cen, quad, off = [two(v) for v in cen8], [two(v) for v in quad8], [two(v) for v in off8]
        plane = lambda z: ext[z, pl.ds(pl.multiple_of(r0 + q0 + RS, 16), 16), pl.ds(l0 + CS, 128)].astype(jnp.float32)
        acc = [jnp.zeros((16, 128), jnp.float32) for _ in range(4)]
        expo = jnp.zeros((16, 128), jnp.float32)
        passed = jnp.ones((16, 128), jnp.float32)
        before, s = plane(0), plane(1)
        for z in range(layers):
            after = plane(z + 2)
            d = after - before
            r = rscr[z, pl.ds(q0, 16), pl.ds(l0, 128)]
            c = cscr[z, pl.ds(q0, 16), pl.ds(l0, 128)]
            light = jnp.abs(d) * lax.rsqrt(d * d + r * r + (c * c + 1.0)) + (0.3 / 0.7)
            bump = []
            for k in range(4):
                u = s - cen[k]
                bump.append(jnp.exp2(u * u * quad[k] + off[k]))
            expo = expo - ((bump[0] + bump[1]) + (bump[2] + bump[3]))
            later = jnp.exp2(expo)
            weight = (passed - later) * light
            for k in range(4):
                acc[k] = acc[k] + weight * bump[k]
            passed = later
            before, s = s, after
        for ch in range(3):
            m = [two(v) for v in mat8[ch]]
            store(ch, q0, l0, (m[0] * acc[0] + m[1] * acc[1]) + (m[2] * acc[2] + m[3] * acc[3]))
        store(3, q0, l0, passed)
        return 0

    lax.fori_loop(0, CH // 16 * tiles, tile, 0)


def kernel(layers_all, vol, front, back, up, down, left, right, cen, wid, col, opa, out,
           ext, cscr, rscr, dcol, drow, sem):
    layers, rows, cols = vol.shape
    mid = (pl.ds(1, layers), pl.ds(RS, rows), pl.ds(CS, cols))
    pairs = [
        (vol, ext.at[mid]),
        (front, ext.at[pl.ds(0, 1), mid[1], mid[2]]),
        (back, ext.at[pl.ds(layers + 1, 1), mid[1], mid[2]]),
        (up, ext.at[mid[0], pl.ds(0, RS), mid[2]]),
        (down, ext.at[mid[0], pl.ds(RS + rows, RS), mid[2]]),
        (left, ext.at[mid[0], mid[1], pl.ds(0, CS)]),
        (right, ext.at[mid[0], mid[1], pl.ds(CS + cols, CS)]),
    ]
    copies = [pltpu.make_async_copy(a, b, sem.at[i]) for i, (a, b) in enumerate(pairs)]
    for c in copies:
        c.start()
    fill_bands(dcol, drow)
    tab = tables(layers_all, cen, wid, col, opa)
    for c in copies:
        c.wait()

    def chunk(j, _):
        r0 = pl.multiple_of(j * CH, CH)

        def store(ch, q0, l0, value):
            out[ch, pl.ds(pl.multiple_of(r0 + q0, 16), 16), pl.ds(l0, 128)] = value

        march_chunk(r0, ext, cscr, rscr, dcol, drow, tab, store)
        return 0

    lax.fori_loop(0, rows // CH, chunk, 0)


def shifted(block, axis, up):
    n = lax.axis_size(axis)
    pairs = [(i, i + 1) for i in range(n - 1)] if up else [(i + 1, i) for i in range(n - 1)]
    return lax.ppermute(block, axis, pairs)


def local(volume, cen, wid, col, opa):
    slabs = lax.axis_size("depth")
    me = lax.axis_index("depth")
    layers, rows, cols = volume.shape
    front = shifted(volume[-1:], "depth", True)
    back = shifted(volume[:1], "depth", False)
    up = shifted(volume[:, -RS:], "imgy", True)
    down = shifted(volume[:, :RS], "imgy", False)
    left = shifted(volume[:, :, -CS:], "imgx", True)
    right = shifted(volume[:, :, :CS], "imgx", False)
    hbm = pl.BlockSpec(memory_space=pl.ANY)
    smem = pl.BlockSpec(memory_space=pltpu.SMEM)
    part = pl.pallas_call(
        functools.partial(kernel, layers * slabs),
        out_shape=jax.ShapeDtypeStruct((4, rows, cols), jnp.float32),
        in_specs=[hbm] * 7 + [smem] * 4,
        out_specs=pl.BlockSpec(memory_space=pltpu.VMEM),
        scratch_shapes=[
            pltpu.VMEM((layers + 2, rows + 2 * RS, cols + 2 * CS), jnp.bfloat16),
            pltpu.VMEM((layers, CH, cols), jnp.float32),
            pltpu.VMEM((layers, CH, cols), jnp.float32),
            pltpu.VMEM((512, 256), jnp.bfloat16),
            pltpu.VMEM((CH, CH + 2 * RS), jnp.bfloat16),
            pltpu.SemaphoreType.DMA((7,)),
        ],
        compiler_params=pltpu.CompilerParams(vmem_limit_bytes=48 * 2**20),
        name="march",
    )(volume, front, back, up, down, left, right, cen, wid, col, opa)
    piece = rows // slabs
    for bit in range(slabs.bit_length() - 1):
        left_pieces = part.shape[1] // piece
        grouped = part.reshape(4, left_pieces // 2, 2, piece, cols)
        own = me // 2**bit % 2
        kept = lax.dynamic_index_in_dim(grouped, own, 2, keepdims=False)
        sent = lax.dynamic_index_in_dim(grouped, 1 - own, 2, keepdims=False)
        got = lax.ppermute(sent, "depth", [(i, i ^ 1 << bit) for i in range(slabs)])
        near = jnp.where(own == 0, kept, got)
        far = jnp.where(own == 0, got, kept)
        part = jnp.concatenate([near[:3] + near[3:] * far[:3], near[3:] * far[3:]], axis=0)
        part = part.reshape(4, left_pieces // 2 * piece, cols)
    return jnp.concatenate([part[:3], 1.0 - part[3:]], axis=0)[:, None]


def solution(mesh):
    return jax.shard_map(
        local,
        mesh=mesh,
        in_specs=(P("depth", "imgy", "imgx"), P(), P(), P(), P()),
        out_specs=P(None, "imgy", "depth", "imgx"),
        check_vma=False,
    )
```

```python
import functools
import math

import jax
import jax.numpy as jnp
from jax import lax
from jax.experimental import pallas as pl
from jax.experimental.pallas import tpu as pltpu
from jax.sharding import PartitionSpec as P

LOG2E = math.log2(math.e)
RS = 16
CS = 128
CH = 32
MU = 4096.0
POWER = 240.0 / math.log2(1.0 + MU)
MESH = pl.DeviceIdType.MESH


def encode(v):
    return jnp.exp2(jnp.log2(1.0 + MU * v) * POWER - 120.0).astype(jnp.bfloat16)


def decode(y):
    return jnp.exp2((jnp.log2(y.astype(jnp.float32)) + 120.0) * (1.0 / POWER)) * (1.0 / MU) - (1.0 / MU)


def fill_bands(dcol, drow):
    k = lax.broadcasted_iota(jnp.int32, dcol.shape, 0)
    j = lax.broadcasted_iota(jnp.int32, dcol.shape, 1)
    dcol[...] = jnp.where(k == j + CS + 1, 1.0, jnp.where(k == j + CS - 1, -1.0, 0.0)).astype(dcol.dtype)
    i = lax.broadcasted_iota(jnp.int32, drow.shape, 0)
    k = lax.broadcasted_iota(jnp.int32, drow.shape, 1)
    drow[...] = jnp.where(k == i + RS + 1, 1.0, jnp.where(k == i + RS - 1, -1.0, 0.0)).astype(drow.dtype)


def total(colors, c):
    t = jnp.full((8, 128), colors[c, 0], jnp.float32)
    for k in range(1, 4):
        t = t + colors[c, k]
    return t


def tables(layers_all, centers, widths, colors, opacity):
    scale = 1.5 / layers_all * LOG2E
    cen, quad, off = [], [], []
    mat = [[], [], []]
    for k in range(4):
        w = jnp.full((8, 128), widths[k], jnp.float32)
        o = jnp.full((8, 128), opacity[k], jnp.float32) * scale
        cen.append(jnp.full((8, 128), centers[k], jnp.float32))
        quad.append(-LOG2E / (w * w))
        off.append(jnp.log2(o))
        for c in range(3):
            mat[c].append(0.7 * colors[c, k] / o / total(colors, c))
    return cen, quad, off, mat


def march_chunk(r0, ext, cscr, rscr, dcol, drow, tab, store):
    layers = ext.shape[0] - 2
    cols = ext.shape[2] - 2 * CS
    for h in range(cols // 256):
        left = ext[1 : layers + 1, pl.ds(r0 + RS, CH), h * 256 : h * 256 + 512].reshape(layers * CH, 512)
        cscr[:, :, h * 256 : h * 256 + 256] = jnp.dot(
            left, dcol[...], preferred_element_type=jnp.float32
        ).reshape(layers, CH, 256)
    for z in range(layers):
        rscr[z] = jnp.dot(
            drow[...], ext[1 + z, pl.ds(r0, CH + 2 * RS), CS : CS + cols], preferred_element_type=jnp.float32
        )
    cen8, quad8, off8, mat8 = tab
    two = lambda v: jnp.concatenate([v, v], axis=0)
    tiles = cols // 128

    def tile(t, _):
        q0 = pl.multiple_of(t // tiles * 16, 16)
        l0 = pl.multiple_of(t % tiles * 128, 128)
        cen, quad, off = [two(v) for v in cen8], [two(v) for v in quad8], [two(v) for v in off8]
        plane = lambda z: ext[z, pl.ds(pl.multiple_of(r0 + q0 + RS, 16), 16), pl.ds(l0 + CS, 128)].astype(jnp.float32)
        acc = [jnp.zeros((16, 128), jnp.float32) for _ in range(4)]
        expo = jnp.zeros((16, 128), jnp.float32)
        passed = jnp.ones((16, 128), jnp.float32)
        before, s = plane(0), plane(1)
        for z in range(layers):
            after = plane(z + 2)
            d = after - before
            r = rscr[z, pl.ds(q0, 16), pl.ds(l0, 128)]
            c = cscr[z, pl.ds(q0, 16), pl.ds(l0, 128)]
            light = jnp.abs(d) * lax.rsqrt(d * d + r * r + (c * c + 1.0)) + (0.3 / 0.7)
            bump = []
            for k in range(4):
                u = s - cen[k]
                bump.append(jnp.exp2(u * u * quad[k] + off[k]))
            expo = expo - ((bump[0] + bump[1]) + (bump[2] + bump[3]))
            later = jnp.exp2(expo)
            weight = (passed - later) * light
            for k in range(4):
                acc[k] = acc[k] + weight * bump[k]
            passed = later
            before, s = s, after
        for ch in range(3):
            m = [two(v) for v in mat8[ch]]
            store(ch, q0, l0, (m[0] * acc[0] + m[1] * acc[1]) + (m[2] * acc[2] + m[3] * acc[3]))
        store(3, q0, l0, passed)
        return 0

    lax.fori_loop(0, CH // 16 * tiles, tile, 0)


def kernel(n, ny, nx, vol, cen, wid, col, opa, out,
           ext, part, cscr, rscr, dcol, drow, sendbuf, recvbuf,
           local_sem, depth_send, depth_recv, side_send, side_recv, row_send, row_recv, swap_send, swap_recv):
    layers, rows, cols = vol.shape
    me, iy, ix = lax.axis_index("depth"), lax.axis_index("imgy"), lax.axis_index("imgx")
    piece = rows // n
    chunks = rows // CH
    rounds = n.bit_length() - 1
    early = piece == CH

    def bit(dev, k):
        return dev // 2**k % 2

    def partner(k):
        return me + (1 - 2 * bit(me, k)) * 2**k

    def order(dev, j):
        if not early:
            return j
        half, quarter = n // 2, n // 4
        kept, i = j // half, j % half
        later, b0, b1 = i // quarter, bit(dev, 0), bit(dev, 1)
        h = 2 * ((i + b0) % quarter) + (1 - b1) * (1 - later) + b1 * later
        return 2 * h + (1 - b0) * (1 - kept) + b0 * kept

    barrier = pltpu.get_barrier_semaphore()

    def greet(dev):
        pl.semaphore_signal(barrier, inc=1, device_id=dev, device_id_type=MESH)

    for k in range(rounds):
        greet({"depth": partner(k)})
    peers = rounds
    other = me + 2 * bit(me, 0) - 1
    for name, at, there in (
        ("depth", other, jnp.logical_and(other >= 0, other < n)),
        ("imgy", iy - 1, iy > 0),
        ("imgy", iy + 1, iy < ny - 1),
        ("imgx", ix - 1, ix > 0),
        ("imgx", ix + 1, ix < nx - 1),
    ):
        pl.when(there)(lambda name=name, at=at: greet({name: at}))
        peers = peers + there.astype(jnp.int32)
    pl.semaphore_wait(barrier, peers)

    mid_z, mid_y, mid_x = pl.ds(1, layers), pl.ds(RS, rows), pl.ds(CS, cols)
    own = pltpu.make_async_copy(vol, ext.at[mid_z, mid_y, mid_x], local_sem)

    def chunk_rows(dev, j):
        return pl.multiple_of(order(dev, j) * CH, CH)

    def depth_copy(side, dev, j):
        r0 = chunk_rows(dev, j)
        return pltpu.make_async_remote_copy(
            src_ref=vol.at[pl.ds((layers - 1) * (1 - side), 1), pl.ds(r0, CH), :],
            dst_ref=ext.at[pl.ds((layers + 1) * side, 1), pl.ds(r0 + RS, CH), mid_x],
            send_sem=depth_send.at[side, j],
            recv_sem=depth_recv.at[side, j],
            device_id={"depth": me + 1 - 2 * side},
            device_id_type=MESH,
        )

    def side_copy(side, j):
        r0 = chunk_rows(me, j)
        return pltpu.make_async_remote_copy(
            src_ref=vol.at[:, pl.ds(r0, CH), pl.ds((cols - CS) * (1 - side), CS)],
            dst_ref=ext.at[mid_z, pl.ds(r0 + RS, CH), pl.ds((cols + CS) * side, CS)],
            send_sem=side_send.at[side, j],
            recv_sem=side_recv.at[side, j],
            device_id={"imgx": ix + 1 - 2 * side},
            device_id_type=MESH,
        )

    def row_copy(side):
        return pltpu.make_async_remote_copy(
            src_ref=vol.at[:, pl.ds((rows - RS) * (1 - side), RS), :],
            dst_ref=ext.at[mid_z, pl.ds((rows + RS) * side, RS), mid_x],
            send_sem=row_send.at[side],
            recv_sem=row_recv.at[side],
            device_id={"imgy": iy + 1 - 2 * side},
            device_id_type=MESH,
        )

    sends = (me < n - 1, me > 0)
    side_sends = (ix < nx - 1, ix > 0)
    row_sends = (iy < ny - 1, iy > 0)

    def start_halos(j):
        for s in range(2):
            pl.when(side_sends[s])(lambda s=s: side_copy(s, j).start())
            pl.when(sends[s])(lambda s=s: depth_copy(s, me + 1 - 2 * s, j).start())

    start_halos(0)
    own.start()
    for s in range(2):
        pl.when(row_sends[s])(lambda s=s: row_copy(s).start())

    def rest(j, _):
        start_halos(j)
        return 0

    lax.fori_loop(1, chunks, rest, 0)

    def clear(region):
        region[...] = jnp.zeros(region.shape, region.dtype)

    for s in range(2):
        pl.when(jnp.logical_not(sends[1 - s]))(lambda s=s: clear(ext.at[pl.ds((layers + 1) * s, 1), mid_y, mid_x]))
        pl.when(jnp.logical_not(side_sends[1 - s]))(
            lambda s=s: clear(ext.at[mid_z, mid_y, pl.ds((cols + CS) * s, CS)]))
        pl.when(jnp.logical_not(row_sends[1 - s]))(
            lambda s=s: clear(ext.at[mid_z, pl.ds((rows + RS) * s, RS), mid_x]))
    fill_bands(dcol, drow)
    tab = tables(layers * n, cen, wid, col, opa)
    own.wait()

    lanes = cols // 128

    def swap_copy(k, h):
        slot = n - n // 2**k + h
        return pltpu.make_async_remote_copy(
            src_ref=sendbuf.at[slot],
            dst_ref=recvbuf.at[slot],
            send_sem=swap_send.at[slot],
            recv_sem=swap_recv.at[slot],
            device_id={"depth": partner(k)},
            device_id_type=MESH,
        )

    def send_piece(p, k):
        h = p // 2 ** (k + 1)
        slot = n - n // 2**k + h
        r0 = pl.multiple_of(p * piece, piece)

        def tile(t, _):
            here = pl.ds(pl.multiple_of(t * 128, 128), 128)
            for ch in range(4):
                v = part[ch, pl.ds(r0, piece), here]
                sendbuf[slot, ch, :, here] = encode(1.0 - v if ch == 3 else v)
            return 0

        lax.fori_loop(0, lanes, tile, 0)
        swap_copy(k, h).start()

    def merge_piece(p, k, last):
        h = p // 2 ** (k + 1)
        slot = n - n // 2**k + h
        r0 = pl.multiple_of(p * piece, piece)
        swap_copy(k, h).wait_recv()
        behind = bit(me, k) == 1

        def tile(t, _):
            here = pl.ds(pl.multiple_of(t * 128, 128), 128)
            mine = [part[ch, pl.ds(r0, piece), here] for ch in range(4)]
            got = [decode(recvbuf[slot, ch, :, here]) for ch in range(4)]
            got[3] = 1.0 - got[3]
            near_t = jnp.where(behind, got[3], mine[3])
            merged = [jnp.where(behind, got[c], mine[c]) + near_t * jnp.where(behind, mine[c], got[c]) for c in range(3)]
            merged.append(mine[3] * got[3])
            for ch in range(4):
                if last:
                    v = 1.0 - merged[3] if ch == 3 else merged[ch] * total(col, ch)[:1]
                    out[ch, 0, :, here] = v
                else:
                    part[ch, pl.ds(r0, piece), here] = merged[ch]
            return 0

        lax.fori_loop(0, lanes, tile, 0)

    def chunk(j, _):
        p = order(me, j)
        r0 = pl.multiple_of(p * CH, CH)
        for s in range(2):
            pl.when(sends[1 - s])(lambda s=s: depth_copy(s, me, j).wait_recv())
            pl.when(side_sends[1 - s])(lambda s=s: side_copy(s, j).wait_recv())
            edge = p == (chunks - 1) * s
            pl.when(jnp.logical_and(row_sends[1 - s], edge))(lambda s=s: row_copy(s).wait_recv())

        def store(ch, q0, l0, value):
            part[ch, pl.ds(pl.multiple_of(r0 + q0, 16), 16), pl.ds(l0, 128)] = value

        march_chunk(r0, ext, cscr, rscr, dcol, drow, tab, store)
        if early:
            pl.when(j < n // 2)(lambda: send_piece(p, 0))
        return 0

    lax.fori_loop(0, chunks, chunk, 0)

    for k in range(rounds):

        def give(h, _, k=k):
            p = me % 2**k + (1 - bit(me, k)) * 2**k + h * 2 ** (k + 1)
            for done in range(k):
                merge_piece(p, done, False)
            send_piece(p, k)
            return 0

        if k > 0 or not early:
            lax.fori_loop(0, n // 2 ** (k + 1), give, 0)
    for k in range(rounds):
        merge_piece(me, k, k == rounds - 1)

    def finish(j, _):
        for s in range(2):
            pl.when(side_sends[s])(lambda s=s: side_copy(s, j).wait_send())
            pl.when(sends[s])(lambda s=s: depth_copy(s, me + 1 - 2 * s, j).wait_send())
        return 0

    lax.fori_loop(0, chunks, finish, 0)
    for s in range(2):
        pl.when(row_sends[s])(lambda s=s: row_copy(s).wait_send())
    for k in range(rounds):

        def sent(h, _, k=k):
            swap_copy(k, h).wait_send()
            return 0

        lax.fori_loop(0, n // 2 ** (k + 1), sent, 0)


def local(volume, cen, wid, col, opa):
    n, ny, nx = lax.axis_size("depth"), lax.axis_size("imgy"), lax.axis_size("imgx")
    layers, rows, cols = volume.shape
    piece = rows // n
    smem = pl.BlockSpec(memory_space=pltpu.SMEM)
    dma = pltpu.SemaphoreType.DMA
    return pl.pallas_call(
        functools.partial(kernel, n, ny, nx),
        out_shape=jax.ShapeDtypeStruct((4, 1, piece, cols), jnp.float32),
        in_specs=[pl.BlockSpec(memory_space=pl.ANY)] + [smem] * 4,
        out_specs=pl.BlockSpec(memory_space=pltpu.VMEM),
        scratch_shapes=[
            pltpu.VMEM((layers + 2, rows + 2 * RS, cols + 2 * CS), jnp.bfloat16),
            pltpu.VMEM((4, rows, cols), jnp.float32),
            pltpu.VMEM((layers, CH, cols), jnp.float32),
            pltpu.VMEM((layers, CH, cols), jnp.float32),
            pltpu.VMEM((512, 256), jnp.bfloat16),
            pltpu.VMEM((CH, CH + 2 * RS), jnp.bfloat16),
            pltpu.VMEM((n - 1, 4, piece, cols), jnp.bfloat16),
            pltpu.VMEM((n - 1, 4, piece, cols), jnp.bfloat16),
            dma,
            dma((2, rows // CH)),
            dma((2, rows // CH)),
            dma((2, rows // CH)),
            dma((2, rows // CH)),
            dma((2,)),
            dma((2,)),
            dma((n - 1,)),
            dma((n - 1,)),
        ],
        compiler_params=pltpu.CompilerParams(
            vmem_limit_bytes=48 * 2**20, collective_id=0, has_side_effects=True
        ),
        name="march_swap",
    )(volume, cen, wid, col, opa)


def solution(mesh):
    return jax.shard_map(
        local,
        mesh=mesh,
        in_specs=(P("depth", "imgy", "imgx"), P(), P(), P(), P()),
        out_specs=P(None, "imgy", "depth", "imgx"),
        check_vma=False,
    )
```

```python
import functools
import math

import jax
import jax.numpy as jnp
from jax import lax
from jax.experimental import pallas as pl
from jax.experimental.pallas import tpu as pltpu
from jax.sharding import PartitionSpec as P

LOG2E = math.log2(math.e)
RS = 16
CS = 128
CH = 32
AHEAD = 3
MU = 4096.0
POWER = 240.0 / math.log2(1.0 + MU)
MESH = pl.DeviceIdType.MESH


def encode(v):
    return jnp.exp2(jnp.log2(1.0 + MU * v) * POWER - 120.0).astype(jnp.bfloat16)


def decode(y):
    return jnp.exp2((jnp.log2(y.astype(jnp.float32)) + 120.0) * (1.0 / POWER)) * (1.0 / MU) - (1.0 / MU)


def fill_bands(dcol, drow):
    k = lax.broadcasted_iota(jnp.int32, dcol.shape, 0)
    j = lax.broadcasted_iota(jnp.int32, dcol.shape, 1)
    dcol[...] = jnp.where(k == j + CS + 1, 1.0, jnp.where(k == j + CS - 1, -1.0, 0.0)).astype(dcol.dtype)
    i = lax.broadcasted_iota(jnp.int32, drow.shape, 0)
    k = lax.broadcasted_iota(jnp.int32, drow.shape, 1)
    drow[...] = jnp.where(k == i + RS + 1, 1.0, jnp.where(k == i + RS - 1, -1.0, 0.0)).astype(drow.dtype)


def total(colors, c):
    t = jnp.full((8, 128), colors[c, 0], jnp.float32)
    for k in range(1, 4):
        t = t + colors[c, k]
    return t


def tables(layers_all, centers, widths, colors, opacity):
    scale = 1.5 / layers_all * LOG2E
    cen, quad, off = [], [], []
    mat = [[], [], []]
    for k in range(4):
        w = jnp.full((8, 128), widths[k], jnp.float32)
        o = jnp.full((8, 128), opacity[k], jnp.float32) * scale
        cen.append(jnp.full((8, 128), centers[k], jnp.float32))
        quad.append(-LOG2E / (w * w))
        off.append(jnp.log2(o))
        for c in range(3):
            mat[c].append(0.7 * colors[c, k] / o / total(colors, c))
    return cen, quad, off, mat


def march_chunk(r0, ext, cscr, rscr, dcol, drow, tab, store):
    layers = ext.shape[0] - 2
    cols = ext.shape[2] - 2 * CS
    for h in range(cols // 256):
        left = ext[1 : layers + 1, pl.ds(r0 + RS, CH), h * 256 : h * 256 + 512].reshape(layers * CH, 512)
        cscr[:, :, h * 256 : h * 256 + 256] = jnp.dot(
            left, dcol[...], preferred_element_type=jnp.float32
        ).reshape(layers, CH, 256)
    for z in range(layers):
        rscr[z] = jnp.dot(
            drow[...], ext[1 + z, pl.ds(r0, CH + 2 * RS), CS : CS + cols], preferred_element_type=jnp.float32
        )
    cen8, quad8, off8, mat8 = tab
    two = lambda v: jnp.concatenate([v, v], axis=0)
    tiles = cols // 128

    def tile(t, _):
        q0 = pl.multiple_of(t // tiles * 16, 16)
        l0 = pl.multiple_of(t % tiles * 128, 128)
        cen, quad, off = [two(v) for v in cen8], [two(v) for v in quad8], [two(v) for v in off8]
        plane = lambda z: ext[z, pl.ds(pl.multiple_of(r0 + q0 + RS, 16), 16), pl.ds(l0 + CS, 128)].astype(jnp.float32)
        acc = [jnp.zeros((16, 128), jnp.float32) for _ in range(4)]
        expo = jnp.zeros((16, 128), jnp.float32)
        passed = jnp.ones((16, 128), jnp.float32)
        before, s = plane(0), plane(1)
        for z in range(layers):
            after = plane(z + 2)
            d = after - before
            r = rscr[z, pl.ds(q0, 16), pl.ds(l0, 128)]
            c = cscr[z, pl.ds(q0, 16), pl.ds(l0, 128)]
            light = jnp.abs(d) * lax.rsqrt(d * d + r * r + (c * c + 1.0)) + (0.3 / 0.7)
            bump = []
            for k in range(4):
                u = s - cen[k]
                bump.append(jnp.exp2(u * u * quad[k] + off[k]))
            expo = expo - ((bump[0] + bump[1]) + (bump[2] + bump[3]))
            later = jnp.exp2(expo)
            weight = (passed - later) * light
            for k in range(4):
                acc[k] = acc[k] + weight * bump[k]
            passed = later
            before, s = s, after
        for ch in range(3):
            m = [two(v) for v in mat8[ch]]
            store(ch, q0, l0, (m[0] * acc[0] + m[1] * acc[1]) + (m[2] * acc[2] + m[3] * acc[3]))
        store(3, q0, l0, passed)
        return 0

    lax.fori_loop(0, CH // 16 * tiles, tile, 0)


def kernel(n, ny, nx, vol, cen_h, wid_h, col_h, opa_h, out, cen, wid, col, opa,
           ext, part, cscr, rscr, dcol, drow, sendbuf, recvbuf,
           local_sem, fetch_sem, depth_send, depth_recv, side_send, side_recv, row_send, row_recv, swap_send, swap_recv):
    layers, rows, cols = vol.shape
    me, iy, ix = lax.axis_index("depth"), lax.axis_index("imgy"), lax.axis_index("imgx")
    piece = rows // n
    chunks = rows // CH
    rounds = n.bit_length() - 1
    early = piece == CH

    def bit(dev, k):
        return dev // 2**k % 2

    def partner(k):
        return me + (1 - 2 * bit(me, k)) * 2**k

    def order(dev, j):
        if not early:
            return j
        edge = (dev % (n - 1) == 0).astype(jnp.int32) * (j < 2).astype(jnp.int32)
        j = j + edge * (1 - 2 * j)
        p = 0
        for k in range(rounds):
            a, b = bit(dev, k), 1 - bit(j, rounds - 1 - k)
            p = p + 2**k * (a + b - 2 * a * b)
        return p

    barrier = pltpu.get_barrier_semaphore()

    def greet(dev):
        pl.semaphore_signal(barrier, inc=1, device_id=dev, device_id_type=MESH)

    for k in range(rounds):
        greet({"depth": partner(k)})
    peers = rounds
    other = me + 2 * bit(me, 0) - 1
    for name, at, there in (
        ("depth", other, jnp.logical_and(other >= 0, other < n)),
        ("imgy", iy - 1, iy > 0),
        ("imgy", iy + 1, iy < ny - 1),
        ("imgx", ix - 1, ix > 0),
        ("imgx", ix + 1, ix < nx - 1),
    ):
        pl.when(there)(lambda name=name, at=at: greet({name: at}))
        peers = peers + there.astype(jnp.int32)
    pl.semaphore_wait(barrier, peers)

    mid_z, mid_y, mid_x = pl.ds(1, layers), pl.ds(RS, rows), pl.ds(CS, cols)
    fetches = [pltpu.make_async_copy(a, b, fetch_sem.at[i]) for i, (a, b) in enumerate(
        ((cen_h, cen), (wid_h, wid), (col_h, col), (opa_h, opa)))]
    own = pltpu.make_async_copy(vol, ext.at[mid_z, mid_y, mid_x], local_sem)

    def chunk_rows(dev, j):
        return pl.multiple_of(order(dev, j) * CH, CH)

    def depth_copy(side, dev, j):
        r0 = chunk_rows(dev, j)
        return pltpu.make_async_remote_copy(
            src_ref=vol.at[pl.ds((layers - 1) * (1 - side), 1), pl.ds(r0, CH), :],
            dst_ref=ext.at[pl.ds((layers + 1) * side, 1), pl.ds(r0 + RS, CH), mid_x],
            send_sem=depth_send.at[side, j],
            recv_sem=depth_recv.at[side, j],
            device_id={"depth": me + 1 - 2 * side},
            device_id_type=MESH,
        )

    def side_copy(side, j):
        r0 = chunk_rows(me, j)
        return pltpu.make_async_remote_copy(
            src_ref=vol.at[:, pl.ds(r0, CH), pl.ds((cols - CS) * (1 - side), CS)],
            dst_ref=ext.at[mid_z, pl.ds(r0 + RS, CH), pl.ds((cols + CS) * side, CS)],
            send_sem=side_send.at[side, j],
            recv_sem=side_recv.at[side, j],
            device_id={"imgx": ix + 1 - 2 * side},
            device_id_type=MESH,
        )

    def row_copy(side):
        return pltpu.make_async_remote_copy(
            src_ref=vol.at[:, pl.ds((rows - RS) * (1 - side), RS), :],
            dst_ref=ext.at[mid_z, pl.ds((rows + RS) * side, RS), mid_x],
            send_sem=row_send.at[side],
            recv_sem=row_recv.at[side],
            device_id={"imgy": iy + 1 - 2 * side},
            device_id_type=MESH,
        )

    sends = (me < n - 1, me > 0)
    side_sends = (ix < nx - 1, ix > 0)
    row_sends = (iy < ny - 1, iy > 0)

    def start_halos(j):
        for s in range(2):
            pl.when(side_sends[s])(lambda s=s: side_copy(s, j).start())
            pl.when(sends[s])(lambda s=s: depth_copy(s, me + 1 - 2 * s, j).start())

    start_halos(jnp.int32(0))
    own.start()
    for copy in fetches:
        copy.start()
    for s in range(2):
        pl.when(row_sends[s])(lambda s=s: row_copy(s).start())

    def rest(j, _):
        start_halos(j)
        return 0

    lax.fori_loop(1, AHEAD, rest, 0)

    def clear(region):
        region[...] = jnp.zeros(region.shape, region.dtype)

    for s in range(2):
        pl.when(jnp.logical_not(sends[1 - s]))(lambda s=s: clear(ext.at[pl.ds((layers + 1) * s, 1), mid_y, mid_x]))
        pl.when(jnp.logical_not(side_sends[1 - s]))(
            lambda s=s: clear(ext.at[mid_z, mid_y, pl.ds((cols + CS) * s, CS)]))
        pl.when(jnp.logical_not(row_sends[1 - s]))(
            lambda s=s: clear(ext.at[mid_z, pl.ds((rows + RS) * s, RS), mid_x]))
    fill_bands(dcol, drow)
    for copy in fetches:
        copy.wait()
    tab = tables(layers * n, cen, wid, col, opa)
    own.wait()

    lanes = cols // 128

    def swap_copy(k, h):
        slot = n - n // 2**k + h
        return pltpu.make_async_remote_copy(
            src_ref=sendbuf.at[slot],
            dst_ref=recvbuf.at[slot],
            send_sem=swap_send.at[slot],
            recv_sem=swap_recv.at[slot],
            device_id={"depth": partner(k)},
            device_id_type=MESH,
        )

    def send_piece(p, k):
        h = p // 2 ** (k + 1)
        slot = n - n // 2**k + h
        r0 = pl.multiple_of(p * piece, piece)

        def tile(t, _):
            here = pl.ds(pl.multiple_of(t * 128, 128), 128)
            for ch in range(4):
                v = part[ch, pl.ds(r0, piece), here]
                sendbuf[slot, ch, :, here] = encode(1.0 - v if ch == 3 else v)
            return 0

        lax.fori_loop(0, lanes, tile, 0)
        swap_copy(k, h).start()

    def merge_piece(p, k, last):
        h = p // 2 ** (k + 1)
        slot = n - n // 2**k + h
        r0 = pl.multiple_of(p * piece, piece)
        swap_copy(k, h).wait_recv()
        behind = bit(me, k) == 1

        def tile(t, _):
            here = pl.ds(pl.multiple_of(t * 128, 128), 128)
            mine = [part[ch, pl.ds(r0, piece), here] for ch in range(4)]
            got = [decode(recvbuf[slot, ch, :, here]) for ch in range(4)]
            got[3] = 1.0 - got[3]
            near_t = jnp.where(behind, got[3], mine[3])
            merged = [jnp.where(behind, got[c], mine[c]) + near_t * jnp.where(behind, mine[c], got[c]) for c in range(3)]
            merged.append(mine[3] * got[3])
            for ch in range(4):
                if last:
                    v = 1.0 - merged[3] if ch == 3 else merged[ch] * total(col, ch)[:1]
                    out[ch, 0, :, here] = v
                else:
                    part[ch, pl.ds(r0, piece), here] = merged[ch]
            return 0

        lax.fori_loop(0, lanes, tile, 0)

    def give_piece(p, k):
        for done in range(k):
            merge_piece(p, done, False)
        send_piece(p, k)

    def chunk(j, _):
        p = order(me, j)
        r0 = pl.multiple_of(p * CH, CH)
        pl.when(j + AHEAD < chunks)(lambda: start_halos(j + AHEAD))
        for s in range(2):
            pl.when(sends[1 - s])(lambda s=s: depth_copy(s, me, j).wait_recv())
            pl.when(side_sends[1 - s])(lambda s=s: side_copy(s, j).wait_recv())
            edge = p == (chunks - 1) * s
            pl.when(jnp.logical_and(row_sends[1 - s], edge))(lambda s=s: row_copy(s).wait_recv())

        def store(ch, q0, l0, value):
            part[ch, pl.ds(pl.multiple_of(r0 + q0, 16), 16), pl.ds(l0, 128)] = value

        march_chunk(r0, ext, cscr, rscr, dcol, drow, tab, store)
        if early:
            for k in range(rounds):
                mine = jnp.logical_and(j >= n - n // 2**k, j < n - n // 2 ** (k + 1))
                pl.when(mine)(lambda k=k: give_piece(p, k))
        return 0

    lax.fori_loop(0, chunks, chunk, 0)

    if not early:
        for k in range(rounds):

            def give(h, _, k=k):
                give_piece(me % 2**k + (1 - bit(me, k)) * 2**k + h * 2 ** (k + 1), k)
                return 0

            lax.fori_loop(0, n // 2 ** (k + 1), give, 0)
    for k in range(rounds):
        merge_piece(me, k, k == rounds - 1)

    def finish(j, _):
        for s in range(2):
            pl.when(side_sends[s])(lambda s=s: side_copy(s, j).wait_send())
            pl.when(sends[s])(lambda s=s: depth_copy(s, me + 1 - 2 * s, j).wait_send())
        return 0

    lax.fori_loop(0, chunks, finish, 0)
    for s in range(2):
        pl.when(row_sends[s])(lambda s=s: row_copy(s).wait_send())
    for k in range(rounds):

        def sent(h, _, k=k):
            swap_copy(k, h).wait_send()
            return 0

        lax.fori_loop(0, n // 2 ** (k + 1), sent, 0)


def local(volume, cen, wid, col, opa):
    n, ny, nx = lax.axis_size("depth"), lax.axis_size("imgy"), lax.axis_size("imgx")
    layers, rows, cols = volume.shape
    piece = rows // n
    dma = pltpu.SemaphoreType.DMA
    return pl.pallas_call(
        functools.partial(kernel, n, ny, nx),
        out_shape=jax.ShapeDtypeStruct((4, 1, piece, cols), jnp.float32),
        in_specs=[pl.BlockSpec(memory_space=pltpu.HBM)] * 5,
        out_specs=pl.BlockSpec(memory_space=pltpu.VMEM),
        scratch_shapes=[
            *(pltpu.SMEM(a.shape, jnp.float32) for a in (cen, wid, col, opa)),
            pltpu.VMEM((layers + 2, rows + 2 * RS, cols + 2 * CS), jnp.bfloat16),
            pltpu.VMEM((4, rows, cols), jnp.float32),
            pltpu.VMEM((layers, CH, cols), jnp.float32),
            pltpu.VMEM((layers, CH, cols), jnp.float32),
            pltpu.VMEM((512, 256), jnp.bfloat16),
            pltpu.VMEM((CH, CH + 2 * RS), jnp.bfloat16),
            pltpu.VMEM((n - 1, 4, piece, cols), jnp.bfloat16),
            pltpu.VMEM((n - 1, 4, piece, cols), jnp.bfloat16),
            dma,
            dma((4,)),
            dma((2, rows // CH)),
            dma((2, rows // CH)),
            dma((2, rows // CH)),
            dma((2, rows // CH)),
            dma((2,)),
            dma((2,)),
            dma((n - 1,)),
            dma((n - 1,)),
        ],
        compiler_params=pltpu.CompilerParams(
            vmem_limit_bytes=48 * 2**20, collective_id=0, has_side_effects=True
        ),
        name="march_swap",
    )(volume, cen, wid, col, opa)


def solution(mesh):
    return jax.shard_map(
        local,
        mesh=mesh,
        in_specs=(P("depth", "imgy", "imgx"), P(), P(), P(), P()),
        out_specs=P(None, "imgy", "depth", "imgx"),
        check_vma=False,
    )
```

```python
import functools
import math

import jax
import jax.numpy as jnp
from jax import lax
from jax.experimental import pallas as pl
from jax.experimental.pallas import tpu as pltpu
from jax.sharding import PartitionSpec as P

LOG2E = math.log2(math.e)
RS = 16
CS = 128
CH = 32
AHEAD = 3
MU = 4096.0
POWER = 240.0 / math.log2(1.0 + MU)
MESH = pl.DeviceIdType.MESH


def encode(v):
    return jnp.exp2(jnp.log2(1.0 + MU * v) * POWER - 120.0).astype(jnp.bfloat16)


def decode(y):
    return jnp.exp2((jnp.log2(y.astype(jnp.float32)) + 120.0) * (1.0 / POWER)) * (1.0 / MU) - (1.0 / MU)


def fill_bands(dcol, drow):
    k = lax.broadcasted_iota(jnp.int32, dcol.shape, 0)
    j = lax.broadcasted_iota(jnp.int32, dcol.shape, 1)
    dcol[...] = jnp.where(k == j + CS + 1, 1.0, jnp.where(k == j + CS - 1, -1.0, 0.0)).astype(dcol.dtype)
    i = lax.broadcasted_iota(jnp.int32, drow.shape, 0)
    k = lax.broadcasted_iota(jnp.int32, drow.shape, 1)
    drow[...] = jnp.where(k == i + RS + 1, 1.0, jnp.where(k == i + RS - 1, -1.0, 0.0)).astype(drow.dtype)


def total(colors, c):
    t = jnp.full((8, 128), colors[c, 0], jnp.float32)
    for k in range(1, 4):
        t = t + colors[c, k]
    return t


def tables(layers_all, centers, widths, colors, opacity):
    scale = 1.5 / layers_all * LOG2E
    cen, quad, off = [], [], []
    mat = [[], [], []]
    for k in range(4):
        w = jnp.full((8, 128), widths[k], jnp.float32)
        o = jnp.full((8, 128), opacity[k], jnp.float32) * scale
        cen.append(jnp.full((8, 128), centers[k], jnp.float32))
        quad.append(-LOG2E / (w * w))
        off.append(jnp.log2(o))
        for c in range(3):
            mat[c].append(0.7 * colors[c, k] / o / total(colors, c))
    return cen, quad, off, mat


def march_chunk(r0, ext, cscr, rscr, dcol, drow, tab, store):
    layers = ext.shape[0] - 2
    cols = ext.shape[2] - 2 * CS
    for h in range(cols // 256):
        left = ext[1 : layers + 1, pl.ds(r0 + RS, CH), h * 256 : h * 256 + 512].reshape(layers * CH, 512)
        cscr[:, :, h * 256 : h * 256 + 256] = jnp.dot(
            left, dcol[...], preferred_element_type=jnp.float32
        ).reshape(layers, CH, 256)
    for z in range(layers):
        rscr[z] = jnp.dot(
            drow[...], ext[1 + z, pl.ds(r0, CH + 2 * RS), CS : CS + cols], preferred_element_type=jnp.float32
        )
    cen8, quad8, off8, mat8 = tab
    two = lambda v: jnp.concatenate([v, v], axis=0)
    tiles = cols // 128

    def tile(t, _):
        q0 = pl.multiple_of(t // tiles * 16, 16)
        l0 = pl.multiple_of(t % tiles * 128, 128)
        cen, quad, off = [two(v) for v in cen8], [two(v) for v in quad8], [two(v) for v in off8]
        plane = lambda z: ext[z, pl.ds(pl.multiple_of(r0 + q0 + RS, 16), 16), pl.ds(l0 + CS, 128)].astype(jnp.float32)
        acc = [jnp.zeros((16, 128), jnp.float32) for _ in range(4)]
        expo = jnp.zeros((16, 128), jnp.float32)
        passed = jnp.ones((16, 128), jnp.float32)
        before, s = plane(0), plane(1)
        for z in range(layers):
            after = plane(z + 2)
            d = after - before
            r = rscr[z, pl.ds(q0, 16), pl.ds(l0, 128)]
            c = cscr[z, pl.ds(q0, 16), pl.ds(l0, 128)]
            light = jnp.abs(d) * lax.rsqrt(d * d + r * r + (c * c + 1.0)) + (0.3 / 0.7)
            bump = []
            for k in range(4):
                u = s - cen[k]
                bump.append(jnp.exp2(u * u * quad[k] + off[k]))
            expo = expo - ((bump[0] + bump[1]) + (bump[2] + bump[3]))
            later = jnp.exp2(expo)
            weight = (passed - later) * light
            for k in range(4):
                acc[k] = acc[k] + weight * bump[k]
            passed = later
            before, s = s, after
        for ch in range(3):
            m = [two(v) for v in mat8[ch]]
            store(ch, q0, l0, (m[0] * acc[0] + m[1] * acc[1]) + (m[2] * acc[2] + m[3] * acc[3]))
        store(3, q0, l0, passed)
        return 0

    lax.fori_loop(0, CH // 16 * tiles, tile, 0)


def kernel(n, ny, nx, vol, cen_h, wid_h, col_h, opa_h, out, cen, wid, col, opa,
           ext, part, cscr, rscr, dcol, drow, sendbuf, recvbuf,
           local_sem, fetch_sem, depth_send, depth_recv, side_send, side_recv, row_send, row_recv, swap_send, swap_recv):
    layers, rows, cols = vol.shape
    me, iy, ix = lax.axis_index("depth"), lax.axis_index("imgy"), lax.axis_index("imgx")
    piece = rows // n
    chunks = rows // CH
    rounds = n.bit_length() - 1
    early = piece == CH

    def bit(dev, k):
        return dev // 2**k % 2

    def partner(k):
        return me + (1 - 2 * bit(me, k)) * 2**k

    def order(dev, j):
        if not early:
            return j
        edge = (dev % (n - 1) == 0).astype(jnp.int32) * (j < 2).astype(jnp.int32)
        j = j + edge * (1 - 2 * j)
        p = 0
        for k in range(rounds):
            a, b = bit(dev, k), 1 - bit(j, rounds - 1 - k)
            p = p + 2**k * (a + b - 2 * a * b)
        return p

    barrier = pltpu.get_barrier_semaphore()

    def greet(dev):
        pl.semaphore_signal(barrier, inc=1, device_id=dev, device_id_type=MESH)

    for k in range(rounds):
        greet({"depth": partner(k)})
    peers = rounds
    other = me + 2 * bit(me, 0) - 1
    for name, at, there in (
        ("depth", other, jnp.logical_and(other >= 0, other < n)),
        ("imgy", iy - 1, iy > 0),
        ("imgy", iy + 1, iy < ny - 1),
        ("imgx", ix - 1, ix > 0),
        ("imgx", ix + 1, ix < nx - 1),
    ):
        pl.when(there)(lambda name=name, at=at: greet({name: at}))
        peers = peers + there.astype(jnp.int32)
    pl.semaphore_wait(barrier, peers)

    mid_z, mid_y, mid_x = pl.ds(1, layers), pl.ds(RS, rows), pl.ds(CS, cols)
    fetches = [pltpu.make_async_copy(a, b, fetch_sem.at[i]) for i, (a, b) in enumerate(
        ((cen_h, cen), (wid_h, wid), (col_h, col), (opa_h, opa)))]
    own = pltpu.make_async_copy(vol, ext.at[mid_z, mid_y, mid_x], local_sem)

    def chunk_rows(dev, j):
        return pl.multiple_of(order(dev, j) * CH, CH)

    def depth_copy(side, dev, j):
        r0 = chunk_rows(dev, j)
        return pltpu.make_async_remote_copy(
            src_ref=vol.at[pl.ds((layers - 1) * (1 - side), 1), pl.ds(r0, CH), :],
            dst_ref=ext.at[pl.ds((layers + 1) * side, 1), pl.ds(r0 + RS, CH), mid_x],
            send_sem=depth_send.at[side, j],
            recv_sem=depth_recv.at[side, j],
            device_id={"depth": me + 1 - 2 * side},
            device_id_type=MESH,
        )

    def side_copy(side, j):
        r0 = chunk_rows(me, j)
        return pltpu.make_async_remote_copy(
            src_ref=vol.at[:, pl.ds(r0, CH), pl.ds((cols - CS) * (1 - side), CS)],
            dst_ref=ext.at[mid_z, pl.ds(r0 + RS, CH), pl.ds((cols + CS) * side, CS)],
            send_sem=side_send.at[side, j],
            recv_sem=side_recv.at[side, j],
            device_id={"imgx": ix + 1 - 2 * side},
            device_id_type=MESH,
        )

    def row_copy(side):
        return pltpu.make_async_remote_copy(
            src_ref=vol.at[:, pl.ds((rows - RS) * (1 - side), RS), :],
            dst_ref=ext.at[mid_z, pl.ds((rows + RS) * side, RS), mid_x],
            send_sem=row_send.at[side],
            recv_sem=row_recv.at[side],
            device_id={"imgy": iy + 1 - 2 * side},
            device_id_type=MESH,
        )

    sends = (me < n - 1, me > 0)
    side_sends = (ix < nx - 1, ix > 0)
    row_sends = (iy < ny - 1, iy > 0)

    def start_halos(j):
        for s in range(2):
            pl.when(side_sends[s])(lambda s=s: side_copy(s, j).start())
            pl.when(sends[s])(lambda s=s: depth_copy(s, me + 1 - 2 * s, j).start())

    start_halos(jnp.int32(0))
    own.start()
    for copy in fetches:
        copy.start()
    for s in range(2):
        pl.when(row_sends[s])(lambda s=s: row_copy(s).start())

    def rest(j, _):
        start_halos(j)
        return 0

    lax.fori_loop(1, AHEAD, rest, 0)

    def clear(region):
        region[...] = jnp.zeros(region.shape, region.dtype)

    for s in range(2):
        pl.when(jnp.logical_not(sends[1 - s]))(lambda s=s: clear(ext.at[pl.ds((layers + 1) * s, 1), mid_y, mid_x]))
        pl.when(jnp.logical_not(side_sends[1 - s]))(
            lambda s=s: clear(ext.at[mid_z, mid_y, pl.ds((cols + CS) * s, CS)]))
        pl.when(jnp.logical_not(row_sends[1 - s]))(
            lambda s=s: clear(ext.at[mid_z, pl.ds((rows + RS) * s, RS), mid_x]))
    fill_bands(dcol, drow)
    for copy in fetches:
        copy.wait()
    tab = tables(layers * n, cen, wid, col, opa)
    own.wait()

    lanes = cols // 128

    def swap_copy(k, h):
        slot = n - n // 2**k + h
        return pltpu.make_async_remote_copy(
            src_ref=sendbuf.at[slot],
            dst_ref=recvbuf.at[slot],
            send_sem=swap_send.at[slot],
            recv_sem=swap_recv.at[slot],
            device_id={"depth": partner(k)},
            device_id_type=MESH,
        )

    def send_piece(p, k):
        h = p // 2 ** (k + 1)
        slot = n - n // 2**k + h
        r0 = pl.multiple_of(p * piece, piece)

        def tile(t, _):
            here = pl.ds(pl.multiple_of(t * 128, 128), 128)
            for ch in range(4):
                v = part[ch, pl.ds(r0, piece), here]
                sendbuf[slot, ch, :, here] = encode(1.0 - v if ch == 3 else v)
            return 0

        lax.fori_loop(0, lanes, tile, 0)
        swap_copy(k, h).start()

    def merge_piece(p, k, last):
        h = p // 2 ** (k + 1)
        slot = n - n // 2**k + h
        r0 = pl.multiple_of(p * piece, piece)
        swap_copy(k, h).wait_recv()
        behind = bit(me, k) == 1

        def tile(t, _):
            here = pl.ds(pl.multiple_of(t * 128, 128), 128)
            mine = [part[ch, pl.ds(r0, piece), here] for ch in range(4)]
            got = [decode(recvbuf[slot, ch, :, here]) for ch in range(4)]
            got[3] = 1.0 - got[3]
            near_t = jnp.where(behind, got[3], mine[3])
            merged = [jnp.where(behind, got[c], mine[c]) + near_t * jnp.where(behind, mine[c], got[c]) for c in range(3)]
            merged.append(mine[3] * got[3])
            for ch in range(4):
                if last:
                    v = 1.0 - merged[3] if ch == 3 else merged[ch] * total(col, ch)[:1]
                    out[ch, 0, :, here] = v
                else:
                    part[ch, pl.ds(r0, piece), here] = merged[ch]
            return 0

        lax.fori_loop(0, lanes, tile, 0)

    def give_piece(p, k):
        for done in range(k):
            merge_piece(p, done, False)
        send_piece(p, k)

    def chunk(j, _):
        p = order(me, j)
        r0 = pl.multiple_of(p * CH, CH)
        pl.when(j + AHEAD < chunks)(lambda: start_halos(j + AHEAD))
        for s in range(2):
            pl.when(sends[1 - s])(lambda s=s: depth_copy(s, me, j).wait_recv())
            pl.when(side_sends[1 - s])(lambda s=s: side_copy(s, j).wait_recv())
            edge = p == (chunks - 1) * s
            pl.when(jnp.logical_and(row_sends[1 - s], edge))(lambda s=s: row_copy(s).wait_recv())

        def store(ch, q0, l0, value):
            part[ch, pl.ds(pl.multiple_of(r0 + q0, 16), 16), pl.ds(l0, 128)] = value

        march_chunk(r0, ext, cscr, rscr, dcol, drow, tab, store)
        if early:
            for k in range(rounds):
                mine = jnp.logical_and(j >= n - n // 2**k, j < n - n // 2 ** (k + 1))
                pl.when(mine)(lambda k=k: give_piece(p, k))
        return 0

    lax.fori_loop(0, chunks, chunk, 0)

    if not early:
        for k in range(rounds):

            def give(h, _, k=k):
                give_piece(me % 2**k + (1 - bit(me, k)) * 2**k + h * 2 ** (k + 1), k)
                return 0

            lax.fori_loop(0, n // 2 ** (k + 1), give, 0)
    for k in range(rounds):
        merge_piece(me, k, k == rounds - 1)

    def finish(j, _):
        for s in range(2):
            pl.when(side_sends[s])(lambda s=s: side_copy(s, j).wait_send())
            pl.when(sends[s])(lambda s=s: depth_copy(s, me + 1 - 2 * s, j).wait_send())
        return 0

    lax.fori_loop(0, chunks, finish, 0)
    for s in range(2):
        pl.when(row_sends[s])(lambda s=s: row_copy(s).wait_send())
    for k in range(rounds):

        def sent(h, _, k=k):
            swap_copy(k, h).wait_send()
            return 0

        lax.fori_loop(0, n // 2 ** (k + 1), sent, 0)


def local(volume, cen, wid, col, opa):
    n, ny, nx = lax.axis_size("depth"), lax.axis_size("imgy"), lax.axis_size("imgx")
    layers, rows, cols = volume.shape
    piece = rows // n
    dma = pltpu.SemaphoreType.DMA
    return pl.pallas_call(
        functools.partial(kernel, n, ny, nx),
        out_shape=jax.ShapeDtypeStruct((4, 1, piece, cols), jnp.float32),
        in_specs=[pl.BlockSpec(memory_space=pltpu.HBM)] * 5,
        out_specs=pl.BlockSpec(memory_space=pltpu.VMEM),
        scratch_shapes=[
            *(pltpu.SMEM(a.shape, jnp.float32) for a in (cen, wid, col, opa)),
            pltpu.VMEM((layers + 2, rows + 2 * RS, cols + 2 * CS), jnp.bfloat16),
            pltpu.VMEM((4, rows, cols), jnp.float32),
            pltpu.VMEM((layers, CH, cols), jnp.float32),
            pltpu.VMEM((layers, CH, cols), jnp.float32),
            pltpu.VMEM((512, 256), jnp.bfloat16),
            pltpu.VMEM((CH, CH + 2 * RS), jnp.bfloat16),
            pltpu.VMEM((n - 1, 4, piece, cols), jnp.bfloat16),
            pltpu.VMEM((n - 1, 4, piece, cols), jnp.bfloat16),
            dma,
            dma((4,)),
            dma((2, rows // CH)),
            dma((2, rows // CH)),
            dma((2, rows // CH)),
            dma((2, rows // CH)),
            dma((2,)),
            dma((2,)),
            dma((n - 1,)),
            dma((n - 1,)),
        ],
        compiler_params=pltpu.CompilerParams(
            vmem_limit_bytes=64 * 2**20, collective_id=0, has_side_effects=True
        ),
        name="march_swap",
    )(volume, cen, wid, col, opa)


def solution(mesh):
    return jax.shard_map(
        local,
        mesh=mesh,
        in_specs=(P("depth", "imgy", "imgx"), P(), P(), P(), P()),
        out_specs=P(None, "imgy", "depth", "imgx"),
        check_vma=False,
    )
```

```python
import functools
import math

import jax
import jax.numpy as jnp
from jax import lax
from jax.experimental import pallas as pl
from jax.experimental.pallas import tpu as pltpu
from jax.sharding import PartitionSpec as P

LOG2E = math.log2(math.e)
RS = 16
CS = 128
CH = 32
AHEAD = 3
MU = 4096.0
POWER = 240.0 / math.log2(1.0 + MU)
MESH = pl.DeviceIdType.MESH


def encode(v):
    return jnp.exp2(jnp.log2(1.0 + MU * v) * POWER - 120.0).astype(jnp.bfloat16)


def decode(y):
    return jnp.exp2((jnp.log2(y.astype(jnp.float32)) + 120.0) * (1.0 / POWER)) * (1.0 / MU) - (1.0 / MU)


def fill_bands(dcol, drow):
    k = lax.broadcasted_iota(jnp.int32, dcol.shape, 0)
    j = lax.broadcasted_iota(jnp.int32, dcol.shape, 1)
    dcol[...] = jnp.where(k == j + CS + 1, 1.0, jnp.where(k == j + CS - 1, -1.0, 0.0)).astype(dcol.dtype)
    i = lax.broadcasted_iota(jnp.int32, drow.shape, 0)
    k = lax.broadcasted_iota(jnp.int32, drow.shape, 1)
    drow[...] = jnp.where(k == i + RS + 1, 1.0, jnp.where(k == i + RS - 1, -1.0, 0.0)).astype(drow.dtype)


def total(colors, c):
    t = jnp.full((8, 128), colors[c, 0], jnp.float32)
    for k in range(1, 4):
        t = t + colors[c, k]
    return t


def tables(layers_all, centers, widths, colors, opacity):
    scale = 1.5 / layers_all * LOG2E
    cen, quad, off = [], [], []
    mat = [[], [], []]
    for k in range(4):
        w = jnp.full((8, 128), widths[k], jnp.float32)
        o = jnp.full((8, 128), opacity[k], jnp.float32) * scale
        cen.append(jnp.full((8, 128), centers[k], jnp.float32))
        quad.append(-LOG2E / (w * w))
        off.append(jnp.log2(o))
        for c in range(3):
            mat[c].append(0.7 * colors[c, k] / o / total(colors, c))
    return cen, quad, off, mat


def march_chunk(r0, ext, cscr, rscr, dcol, drow, tab, ready, store):
    layers = ext.shape[0] - 2
    cols = ext.shape[2] - 2 * CS
    for h in range(cols // 256):
        left = ext[1 : layers + 1, pl.ds(r0 + RS, CH), h * 256 : h * 256 + 512].reshape(layers * CH, 512)
        cscr[:, :, h * 256 : h * 256 + 256] = jnp.dot(
            left, dcol[...], preferred_element_type=jnp.float32
        ).reshape(layers, CH, 256)
    for z in range(layers):
        rscr[z] = jnp.dot(
            drow[...], ext[1 + z, pl.ds(r0, CH + 2 * RS), CS : CS + cols], preferred_element_type=jnp.float32
        )
    ready()
    cen8, quad8, off8, mat8 = tab
    two = lambda v: jnp.concatenate([v, v], axis=0)
    tiles = cols // 128

    def tile(t, _):
        q0 = pl.multiple_of(t // tiles * 16, 16)
        l0 = pl.multiple_of(t % tiles * 128, 128)
        cen, quad, off = [two(v) for v in cen8], [two(v) for v in quad8], [two(v) for v in off8]
        plane = lambda z: ext[z, pl.ds(pl.multiple_of(r0 + q0 + RS, 16), 16), pl.ds(l0 + CS, 128)].astype(jnp.float32)
        acc = [jnp.zeros((16, 128), jnp.float32) for _ in range(4)]
        expo = jnp.zeros((16, 128), jnp.float32)
        passed = jnp.ones((16, 128), jnp.float32)
        before, s = plane(0), plane(1)
        for z in range(layers):
            after = plane(z + 2)
            d = after - before
            r = rscr[z, pl.ds(q0, 16), pl.ds(l0, 128)]
            c = cscr[z, pl.ds(q0, 16), pl.ds(l0, 128)]
            light = jnp.abs(d) * lax.rsqrt(d * d + r * r + (c * c + 1.0)) + (0.3 / 0.7)
            bump = []
            for k in range(4):
                u = s - cen[k]
                bump.append(jnp.exp2(u * u * quad[k] + off[k]))
            expo = expo - ((bump[0] + bump[1]) + (bump[2] + bump[3]))
            later = jnp.exp2(expo)
            weight = (passed - later) * light
            for k in range(4):
                acc[k] = acc[k] + weight * bump[k]
            passed = later
            before, s = s, after
        for ch in range(3):
            m = [two(v) for v in mat8[ch]]
            store(ch, q0, l0, (m[0] * acc[0] + m[1] * acc[1]) + (m[2] * acc[2] + m[3] * acc[3]))
        store(3, q0, l0, passed)
        return 0

    lax.fori_loop(0, CH // 16 * tiles, tile, 0, unroll=2)


def kernel(n, ny, nx, vol, cen_h, wid_h, col_h, opa_h, out, cen, wid, col, opa,
           ext, part, cscr, rscr, dcol, drow, sendbuf, recvbuf,
           local_sem, fetch_sem, depth_send, depth_recv, side_send, side_recv, row_send, row_recv, swap_send, swap_recv):
    layers, rows, cols = vol.shape
    me, iy, ix = lax.axis_index("depth"), lax.axis_index("imgy"), lax.axis_index("imgx")
    piece = rows // n
    chunks = rows // CH
    rounds = n.bit_length() - 1
    early = piece == CH

    def bit(dev, k):
        return dev // 2**k % 2

    def partner(k):
        return me + (1 - 2 * bit(me, k)) * 2**k

    def order(dev, j):
        if not early:
            return j
        edge = (dev % (n - 1) == 0).astype(jnp.int32) * (j < 2).astype(jnp.int32)
        j = j + edge * (1 - 2 * j)
        p = 0
        for k in range(rounds):
            a, b = bit(dev, k), 1 - bit(j, rounds - 1 - k)
            p = p + 2**k * (a + b - 2 * a * b)
        return p

    barrier = pltpu.get_barrier_semaphore()

    def greet(dev):
        pl.semaphore_signal(barrier, inc=1, device_id=dev, device_id_type=MESH)

    for k in range(rounds):
        greet({"depth": partner(k)})
    peers = rounds
    other = me + 2 * bit(me, 0) - 1
    for name, at, there in (
        ("depth", other, jnp.logical_and(other >= 0, other < n)),
        ("imgy", iy - 1, iy > 0),
        ("imgy", iy + 1, iy < ny - 1),
        ("imgx", ix - 1, ix > 0),
        ("imgx", ix + 1, ix < nx - 1),
    ):
        pl.when(there)(lambda name=name, at=at: greet({name: at}))
        peers = peers + there.astype(jnp.int32)
    pl.semaphore_wait(barrier, peers)

    mid_z, mid_y, mid_x = pl.ds(1, layers), pl.ds(RS, rows), pl.ds(CS, cols)
    fetches = [pltpu.make_async_copy(a, b, fetch_sem.at[i]) for i, (a, b) in enumerate(
        ((cen_h, cen), (wid_h, wid), (col_h, col), (opa_h, opa)))]
    own = pltpu.make_async_copy(vol, ext.at[mid_z, mid_y, mid_x], local_sem)

    def chunk_rows(dev, j):
        return pl.multiple_of(order(dev, j) * CH, CH)

    def depth_copy(side, dev, j):
        r0 = chunk_rows(dev, j)
        return pltpu.make_async_remote_copy(
            src_ref=vol.at[pl.ds((layers - 1) * (1 - side), 1), pl.ds(r0, CH), :],
            dst_ref=ext.at[pl.ds((layers + 1) * side, 1), pl.ds(r0 + RS, CH), mid_x],
            send_sem=depth_send.at[side, j],
            recv_sem=depth_recv.at[side, j],
            device_id={"depth": me + 1 - 2 * side},
            device_id_type=MESH,
        )

    def side_copy(side, j):
        r0 = chunk_rows(me, j)
        return pltpu.make_async_remote_copy(
            src_ref=vol.at[:, pl.ds(r0, CH), pl.ds((cols - CS) * (1 - side), CS)],
            dst_ref=ext.at[mid_z, pl.ds(r0 + RS, CH), pl.ds((cols + CS) * side, CS)],
            send_sem=side_send.at[side, j],
            recv_sem=side_recv.at[side, j],
            device_id={"imgx": ix + 1 - 2 * side},
            device_id_type=MESH,
        )

    def row_copy(side):
        return pltpu.make_async_remote_copy(
            src_ref=vol.at[:, pl.ds((rows - RS) * (1 - side), RS), :],
            dst_ref=ext.at[mid_z, pl.ds((rows + RS) * side, RS), mid_x],
            send_sem=row_send.at[side],
            recv_sem=row_recv.at[side],
            device_id={"imgy": iy + 1 - 2 * side},
            device_id_type=MESH,
        )

    sends = (me < n - 1, me > 0)
    side_sends = (ix < nx - 1, ix > 0)
    row_sends = (iy < ny - 1, iy > 0)

    def start_halos(j):
        for s in range(2):
            pl.when(side_sends[s])(lambda s=s: side_copy(s, j).start())
            pl.when(sends[s])(lambda s=s: depth_copy(s, me + 1 - 2 * s, j).start())

    start_halos(jnp.int32(0))
    own.start()
    for copy in fetches:
        copy.start()
    for s in range(2):
        pl.when(row_sends[s])(lambda s=s: row_copy(s).start())

    def rest(j, _):
        start_halos(j)
        return 0

    lax.fori_loop(1, AHEAD, rest, 0)

    def clear(region):
        region[...] = jnp.zeros(region.shape, region.dtype)

    for s in range(2):
        pl.when(jnp.logical_not(sends[1 - s]))(lambda s=s: clear(ext.at[pl.ds((layers + 1) * s, 1), mid_y, mid_x]))
        pl.when(jnp.logical_not(side_sends[1 - s]))(
            lambda s=s: clear(ext.at[mid_z, mid_y, pl.ds((cols + CS) * s, CS)]))
        pl.when(jnp.logical_not(row_sends[1 - s]))(
            lambda s=s: clear(ext.at[mid_z, pl.ds((rows + RS) * s, RS), mid_x]))
    fill_bands(dcol, drow)
    for copy in fetches:
        copy.wait()
    tab = tables(layers * n, cen, wid, col, opa)
    own.wait()

    lanes = cols // 128

    def swap_copy(k, h):
        slot = n - n // 2**k + h
        return pltpu.make_async_remote_copy(
            src_ref=sendbuf.at[slot],
            dst_ref=recvbuf.at[slot],
            send_sem=swap_send.at[slot],
            recv_sem=swap_recv.at[slot],
            device_id={"depth": partner(k)},
            device_id_type=MESH,
        )

    def send_piece(p, k):
        h = p // 2 ** (k + 1)
        slot = n - n // 2**k + h
        r0 = pl.multiple_of(p * piece, piece)

        def tile(t, _):
            here = pl.ds(pl.multiple_of(t * 128, 128), 128)
            for ch in range(4):
                v = part[ch, pl.ds(r0, piece), here]
                sendbuf[slot, ch, :, here] = encode(1.0 - v if ch == 3 else v)
            return 0

        lax.fori_loop(0, lanes, tile, 0)
        swap_copy(k, h).start()

    def merge_piece(p, k, last):
        h = p // 2 ** (k + 1)
        slot = n - n // 2**k + h
        r0 = pl.multiple_of(p * piece, piece)
        swap_copy(k, h).wait_recv()
        behind = bit(me, k) == 1

        def tile(t, _):
            here = pl.ds(pl.multiple_of(t * 128, 128), 128)
            mine = [part[ch, pl.ds(r0, piece), here] for ch in range(4)]
            got = [decode(recvbuf[slot, ch, :, here]) for ch in range(4)]
            got[3] = 1.0 - got[3]
            near_t = jnp.where(behind, got[3], mine[3])
            merged = [jnp.where(behind, got[c], mine[c]) + near_t * jnp.where(behind, mine[c], got[c]) for c in range(3)]
            merged.append(mine[3] * got[3])
            for ch in range(4):
                if last:
                    v = 1.0 - merged[3] if ch == 3 else merged[ch] * total(col, ch)[:1]
                    out[ch, 0, :, here] = v
                else:
                    part[ch, pl.ds(r0, piece), here] = merged[ch]
            return 0

        lax.fori_loop(0, lanes, tile, 0)

    def give_piece(p, k):
        for done in range(k):
            merge_piece(p, done, False)
        send_piece(p, k)

    def chunk(j, _):
        p = order(me, j)
        r0 = pl.multiple_of(p * CH, CH)
        pl.when(j + AHEAD < chunks)(lambda: start_halos(j + AHEAD))
        for s in range(2):
            pl.when(side_sends[1 - s])(lambda s=s: side_copy(s, j).wait_recv())
            edge = p == (chunks - 1) * s
            pl.when(jnp.logical_and(row_sends[1 - s], edge))(lambda s=s: row_copy(s).wait_recv())

        def ready():
            for s in range(2):
                pl.when(sends[1 - s])(lambda s=s: depth_copy(s, me, j).wait_recv())

        def store(ch, q0, l0, value):
            part[ch, pl.ds(pl.multiple_of(r0 + q0, 16), 16), pl.ds(l0, 128)] = value

        march_chunk(r0, ext, cscr, rscr, dcol, drow, tab, ready, store)
        if early:
            for k in range(rounds):
                mine = jnp.logical_and(j >= n - n // 2**k, j < n - n // 2 ** (k + 1))
                pl.when(mine)(lambda k=k: give_piece(p, k))
        return 0

    lax.fori_loop(0, chunks, chunk, 0)

    if not early:
        for k in range(rounds):

            def give(h, _, k=k):
                give_piece(me % 2**k + (1 - bit(me, k)) * 2**k + h * 2 ** (k + 1), k)
                return 0

            lax.fori_loop(0, n // 2 ** (k + 1), give, 0)
    for k in range(rounds):
        merge_piece(me, k, k == rounds - 1)

    def finish(j, _):
        for s in range(2):
            pl.when(side_sends[s])(lambda s=s: side_copy(s, j).wait_send())
            pl.when(sends[s])(lambda s=s: depth_copy(s, me + 1 - 2 * s, j).wait_send())
        return 0

    lax.fori_loop(0, chunks, finish, 0)
    for s in range(2):
        pl.when(row_sends[s])(lambda s=s: row_copy(s).wait_send())
    for k in range(rounds):

        def sent(h, _, k=k):
            swap_copy(k, h).wait_send()
            return 0

        lax.fori_loop(0, n // 2 ** (k + 1), sent, 0)


def local(volume, cen, wid, col, opa):
    n, ny, nx = lax.axis_size("depth"), lax.axis_size("imgy"), lax.axis_size("imgx")
    layers, rows, cols = volume.shape
    piece = rows // n
    dma = pltpu.SemaphoreType.DMA
    return pl.pallas_call(
        functools.partial(kernel, n, ny, nx),
        out_shape=jax.ShapeDtypeStruct((4, 1, piece, cols), jnp.float32),
        in_specs=[pl.BlockSpec(memory_space=pltpu.HBM)] * 5,
        out_specs=pl.BlockSpec(memory_space=pltpu.VMEM),
        scratch_shapes=[
            *(pltpu.SMEM(a.shape, jnp.float32) for a in (cen, wid, col, opa)),
            pltpu.VMEM((layers + 2, rows + 2 * RS, cols + 2 * CS), jnp.bfloat16),
            pltpu.VMEM((4, rows, cols), jnp.float32),
            pltpu.VMEM((layers, CH, cols), jnp.float32),
            pltpu.VMEM((layers, CH, cols), jnp.float32),
            pltpu.VMEM((512, 256), jnp.bfloat16),
            pltpu.VMEM((CH, CH + 2 * RS), jnp.bfloat16),
            pltpu.VMEM((n - 1, 4, piece, cols), jnp.bfloat16),
            pltpu.VMEM((n - 1, 4, piece, cols), jnp.bfloat16),
            dma,
            dma((4,)),
            dma((2, rows // CH)),
            dma((2, rows // CH)),
            dma((2, rows // CH)),
            dma((2, rows // CH)),
            dma((2,)),
            dma((2,)),
            dma((n - 1,)),
            dma((n - 1,)),
        ],
        compiler_params=pltpu.CompilerParams(
            vmem_limit_bytes=64 * 2**20, collective_id=0, has_side_effects=True
        ),
        name="march_swap",
    )(volume, cen, wid, col, opa)


def solution(mesh):
    return jax.shard_map(
        local,
        mesh=mesh,
        in_specs=(P("depth", "imgy", "imgx"), P(), P(), P(), P()),
        out_specs=P(None, "imgy", "depth", "imgx"),
        check_vma=False,
    )
```
